32 devices in a mesh: blk: 8 (over y, x, core), red: 4 (over z).
Axes of the slice: x: 2, y: 2, z: 4, core: 2. Of those that a mesh axis runs over, the one named last changes fastest.
Arguments:
- x_now: bfloat16 [512, 131072], P('blk', 'red'), may hold values from -6 to 6
- x_prev: float32 [512, 131072], P('blk', 'red'), may hold values from -6 to 6
- density: float32 [512, 131072], P('blk', 'red'), may hold values from -6 to 6
- coeffs: float32 [8], replicated, may hold values from -1 to 1
- potential: int32 [32], P('blk'), may hold values from 0 to 7
- h_tiles: bfloat16 [8, 48, 256, 256], P('blk', 'red'), may hold values from -0.1796875 to 0.1796875
- tile_rows: int32 [8, 48], P('blk', 'red'), may hold values from 0 to 63
- tile_cols: int32 [8, 48], P('blk', 'red'), may hold values from 0 to 127, as said below
- tile_counts: int32 [8, 4], P('blk', 'red'), may hold values from 3 to 12, as said below
Outputs:
- x_next: float32 [512, 131072], P('blk', 'red')
- density_out: float32 [512, 131072], P('blk', 'red')
The draws below stay inside these ranges and needn't reach their ends.
Inputs may be any that keep to these rules, and one draw needn't show every extreme that they name: `tile_cols`: block column within the group; the live slots of one panel and group name distinct positions (row, column). `tile_counts`: at most 12 live slots; some panel and group is full in every draw.
All inputs are finite; a program needn't handle non-finite values.
Results may differ from the reference program's by a relative error of at most 0.005.
Values may be sent and summed in bfloat16 or wider, within the bound.
No kernel may reach another device: no remote copies, remote signals or barrier semaphores. Data moves between devices by JAX's collectives and lax.ppermute only.
A program may use at most 128 MiB of HBM per device.

```python
import jax
import jax.numpy as jnp
from jax import lax

BS = 256
ORDER = 131072
NMU = 8
SLAB_W = 16
CAP = 12
NB = 512
RB = 64
CB = 128
SLABS = 32
COLS = 512
N_BLK = 8
N_RED = 4


def tile_layout(key):
    slices = N_BLK * N_RED
    places = RB * CB
    scores = jax.random.randint(jax.random.fold_in(key, 11), (slices, places), 0, 100000) * places + jnp.arange(places, dtype=jnp.int32)[None, :]
    unused, picks = lax.top_k(scores, CAP)
    picks = picks.astype(jnp.int32)
    row_ids = (picks // CB).reshape(N_BLK, N_RED * CAP)
    col_ids = (picks % CB).reshape(N_BLK, N_RED * CAP)
    return (row_ids, col_ids)


def draw_tile_rows(key, part):
    return tile_layout(key)[0]


def draw_tile_cols(key, part):
    return tile_layout(key)[1]


def draw_tile_counts(key, part):
    slices = N_BLK * N_RED
    counts = jax.random.randint(jax.random.fold_in(key, 23), (slices,), max(1, CAP // 4), CAP + 1)
    forced = jax.random.randint(jax.random.fold_in(key, 29), (), 0, slices)
    counts = jnp.where(jnp.arange(slices, dtype=jnp.int32) == forced, CAP, counts)
    return counts.astype(jnp.int32).reshape(N_BLK, N_RED)


def plant(values, rng, smallest, top_value):
    extent = values.shape
    spot = [jax.random.randint(jax.random.fold_in(rng, axis), (), 0, extent[axis]) for axis in range(len(extent))]
    values = values.at[tuple(spot)].set(smallest)
    longest = extent.index(max(extent))
    spot[longest] = (spot[longest] + 1) % extent[longest]
    return values.at[tuple(spot)].set(top_value)


def levels(rng, dims, split, smallest, top_value):
    gain, own = 1.0, jax.random.fold_in(rng, 6)
    for dim, blocks in split:
        steps = jnp.exp(jax.random.uniform(jax.random.fold_in(own, dim), (blocks,), jnp.float32, smallest / len(split), top_value / len(split)))
        gain = gain * jnp.repeat(steps, dims[dim] // blocks).reshape([-1 if axis == dim else 1 for axis in range(len(dims))])
    return gain


def noise(own_key, dims, scale, reach, pieces=(), kind=jnp.bfloat16):
    factor_of = levels(own_key, dims, pieces, -0.22, 0.18) if pieces else 1.0
    entries = jax.random.normal(own_key, dims, jnp.float32) * scale * factor_of
    return jnp.minimum(jnp.maximum(entries, -reach), reach).astype(kind)


def setup_inputs(seed: int = 0) -> dict:
    key_list = jax.random.split(jax.random.key(seed), 10)
    x_now = noise(key_list[0], (COLS, ORDER), 1.0, 6.0, ((0, 8), (1, 4)))
    x_prev = noise(key_list[1], (COLS, ORDER), 1.0, 6.0, ((0, 8), (1, 4)), jnp.float32)
    density = noise(key_list[2], (COLS, ORDER), 1.0, 6.0, ((0, 8), (1, 4)), jnp.float32)
    coeffs = jnp.clip(jax.random.uniform(key_list[3], (NMU,), jnp.float32, -1.0, 1.0), -1.0, 1.0)
    potential = plant(jax.random.randint(key_list[4], (SLABS,), 0, NMU), jax.random.fold_in(key_list[4], 1), 0, NMU - 1).astype(jnp.int32)
    h_tiles = noise(key_list[5], (N_BLK, N_RED * CAP, BS, BS), 0.03, 0.1796875, ((0, 8), (1, 4)))
    tile_rows = draw_tile_rows(jax.random.fold_in(key_list[9], 71), 0)
    tile_cols = draw_tile_cols(jax.random.fold_in(key_list[9], 71), 0)
    tile_counts = draw_tile_counts(jax.random.fold_in(key_list[9], 71), 0)
    return {"x_now": x_now, "x_prev": x_prev, "density": density, "coeffs": coeffs, "potential": potential, "h_tiles": h_tiles, "tile_rows": tile_rows, "tile_cols": tile_cols, "tile_counts": tile_counts}


def group_partial(x_blocks, tile_data, row_ids, col_ids, live_count, group):
    def one_panel(inputs):
        panel_tiles, panel_rows, panel_cols, panel_count = inputs
        picked = jnp.take(x_blocks, group * CB + panel_cols, axis=1).astype(jnp.float32)
        product = jnp.einsum("vck,cik->cvi", picked, panel_tiles.astype(jnp.float32))
        is_live = jnp.arange(CAP, dtype=jnp.int32) < panel_count
        placing = ((panel_rows[:, None] == jnp.arange(RB, dtype=jnp.int32)[None, :]) & is_live[:, None]).astype(jnp.float32)
        return jnp.einsum("cr,cvi->vri", placing, product, precision=lax.Precision.HIGHEST)

    stacked = lax.map(one_panel, (tile_data, row_ids, col_ids, live_count))
    return jnp.transpose(stacked, (1, 0, 2, 3)).reshape(COLS, ORDER)


def reference(x_now, x_prev, density, coeffs, potential, h_tiles, tile_rows, tile_cols, tile_counts):
    x_blocks = x_now.reshape(COLS, NB, BS)
    product = jnp.zeros((COLS, ORDER), jnp.float32)
    for group in range(N_RED):
        lower = group * CAP
        upper = lower + CAP
        partial_value = group_partial(x_blocks, h_tiles[:, lower:upper], tile_rows[:, lower:upper], tile_cols[:, lower:upper], tile_counts[:, group], group)
        rounded = lax.optimization_barrier(partial_value.astype(jnp.bfloat16))
        product = product + rounded.astype(jnp.float32)
    x_next = 2.0 * product - x_prev
    picking = (potential[:, None] == jnp.arange(NMU, dtype=jnp.int32)[None, :]).astype(jnp.float32)
    slab_coef = jnp.sum(picking * coeffs[None, :], axis=1)
    column_coef = jnp.repeat(slab_coef, SLAB_W)
    density_out = density + column_coef[:, None] * x_next
    return x_next, density_out
```

```python
import functools

import jax
import jax.numpy as jnp
from jax import lax
from jax.experimental import pallas as pl
from jax.experimental.pallas import tpu as pltpu
from jax.sharding import Mesh, PartitionSpec as P

SHARES = (4, 4, 4)
DIRECT = (False, True, False)

SMEM = pl.BlockSpec(memory_space=pltpu.SMEM)
VMEM = pl.BlockSpec(memory_space=pltpu.VMEM)
ANY = pl.BlockSpec(memory_space=pl.ANY)


def chunk_sizes(capacity):
    total = sum(SHARES)
    if capacity % total == 0:
        return [part * capacity // total for part in SHARES]
    return [capacity]


def flip_slice(value, bits):
    count = 2 * lax.axis_size("red")
    return lax.ppermute(value, ("core", "red"), [(i, i ^ bits) for i in range(count)])


def flip_chip(value, bits):
    return lax.ppermute(value, "chip", [(i, i ^ bits) for i in range(lax.axis_size("chip"))])


def spread(own, chips):
    pieces = {0: [own]}
    bits = [1 << b for b in range(chips.bit_length() - 1)]
    half = own.shape[0] // 2
    halves = {}
    for bit in bits:
        whole = flip_chip(own, bit)
        pieces[bit] = [whole]
        halves[bit] = (whole[:half], whole[half:])
    direct = [pieces[bit][0] for bit in bits]
    for distance in sorted(range(chips), key=lambda d: (bin(d).count("1"), d)):
        if distance not in pieces:
            low = distance & -distance
            high = 1 << (distance.bit_length() - 1)
            first = flip_chip(halves[distance ^ high][0], high)
            second = flip_chip(halves[distance ^ low][1], low)
            halves[distance] = (first, second)
            pieces[distance] = [first, second]
    return pieces, direct


def products_kernel(layout, chips, reds, capacity, base, size, per_red, direct, *refs):
    place, mine, other = refs[:3]
    facts = refs[3 : 3 + chips]
    tiles = refs[3 + chips : 3 + chips + len(layout)]
    rest = refs[3 + chips + len(layout) :]
    if direct:
        outs, (out, picked, sems, out_sems) = rest[: 2 * reds], rest[2 * reds :]
    else:
        out, picked, sems = rest
    rows = mine.shape[0]
    width = tiles[0].shape[-1]
    chip, core, red = place[0], place[1], place[2]

    jobs = []
    for number, (distance, offset, count) in enumerate(layout):
        for local in range(count):
            jobs.append((distance, offset + local, number, local))

    def fetch(index):
        distance, slot, _, _ = jobs[index]
        column = facts[distance][0, capacity + base + slot]
        start = pl.multiple_of(column * width, width)
        return [
            pltpu.make_async_copy(
                which.at[:, pl.ds(start, width)],
                picked.at[index, pl.ds(side * rows, rows), :],
                sems.at[index, side],
            )
            for side, which in enumerate((mine, other))
        ]

    for index in range(len(jobs)):
        for copy in fetch(index):
            copy.start()
    for index in range(len(jobs)):
        for copy in fetch(index):
            copy.wait()
    for index, (distance, slot, number, local) in enumerate(jobs):
        result = lax.dot_general(
            picked[index],
            tiles[number][local],
            (((1,), (1,)), ((), ())),
            preferred_element_type=jnp.float32,
        ).astype(out.dtype)
        target_chip = jnp.bitwise_xor(chip, distance)
        target = target_chip // per_red
        row = (target_chip % per_red) * size + slot
        if direct:
            away = jnp.bitwise_xor(target, red)
            out[away, row] = result[:rows]
            out[reds + away, row] = result[rows:]
        else:
            out[core * reds + target, row] = result[:rows]
            out[(1 - core) * reds + target, row] = result[rows:]
    if direct:
        copies = [
            pltpu.make_async_copy(out.at[away], outs[away], out_sems.at[away])
            for away in range(2 * reds)
        ]
        for copy in copies:
            copy.start()
        for copy in copies:
            copy.wait()


def products(place, mine, other, facts, pieces, chips, reds, capacity, base, size, per_red, direct):
    layout, tiles = [], []
    for distance in sorted(pieces):
        offset = 0
        for array in pieces[distance]:
            layout.append((distance, offset, array.shape[0]))
            tiles.append(array)
            offset += array.shape[0]
    rows = mine.shape[0]
    width = tiles[0].shape[-1]
    jobs = chips * size
    one = (per_red * size, rows, width)
    scratch = [
        pltpu.VMEM((jobs, 2 * rows, width), jnp.bfloat16),
        pltpu.SemaphoreType.DMA((jobs, 2)),
    ]
    if direct:
        out_shape = [jax.ShapeDtypeStruct(one, jnp.bfloat16)] * (2 * reds)
        out_specs = [ANY] * (2 * reds)
        scratch = [pltpu.VMEM((2 * reds, *one), jnp.bfloat16)] + scratch
        scratch.append(pltpu.SemaphoreType.DMA((2 * reds,)))
    else:
        out_shape = jax.ShapeDtypeStruct((2 * reds, *one), jnp.bfloat16)
        out_specs = VMEM
    return pl.pallas_call(
        functools.partial(
            products_kernel, tuple(layout), chips, reds, capacity, base, size, per_red, direct
        ),
        out_shape=out_shape,
        in_specs=[SMEM, ANY, ANY] + [SMEM] * chips + [VMEM] * len(tiles),
        out_specs=out_specs,
        scratch_shapes=scratch,
    )(place, mine, other, *[facts[d] for d in range(chips)], *tiles)


def plan_kernel(sizes, directs, groups, reds, per_red, capacity, row_blocks, meta, place, table, last):
    core, red = place[1], place[2]

    def clear(i, carry):
        last[0, i] = -1
        last[1, i] = -1
        return carry

    lax.fori_loop(0, last.shape[1], clear, 0)
    position = jnp.int32(0)
    base = 0
    bound = 0
    for number, (size, direct) in enumerate(zip(sizes, directs)):
        if any(number == group[0] for group in groups):
            opening = position
        for away in range(2 * reds):
            source_core, source_red = away // reds, away % reds
            if direct:
                source_core = jnp.bitwise_xor(core, source_core)
                source_red = jnp.bitwise_xor(red, source_red)
            table[4, bound] = position
            bound += 1
            for local in range(per_red):
                panel = 2 * (red * per_red + local) + source_core
                source = panel * reds + source_red
                live = jnp.clip(meta[source, 2 * capacity] - base, 0, size)

                def enter(slot, position, local=local, source=source, source_core=source_core, base=base, size=size, opening=opening):
                    block = (2 * local + source_core) * row_blocks + meta[source, base + slot]
                    first, latest = last[0, block], last[1, block]
                    seen = first >= opening
                    lead = jnp.where(seen, first, position)
                    table[0, position] = block
                    table[1, position] = lead
                    table[2, position] = 1
                    table[3, position] = local * size + slot
                    last[0, block] = lead
                    last[1, block] = position

                    @pl.when(seen)
                    def _():
                        table[2, latest] = 0

                    return position + 1

                position = lax.fori_loop(0, live, enter, position)
        base += size
    table[4, bound] = position


def plan(meta, place, sizes, directs, groups, reds, per_red, capacity, row_blocks):
    items = max(2 * reds * per_red * capacity, 2 * reds * len(sizes) + 1)
    return pl.pallas_call(
        functools.partial(
            plan_kernel, tuple(sizes), tuple(directs), groups, reds, per_red, capacity, row_blocks
        ),
        out_shape=jax.ShapeDtypeStruct((5, items), jnp.int32),
        in_specs=[SMEM, SMEM],
        out_specs=SMEM,
        scratch_shapes=[pltpu.SMEM((2, 2 * per_red * row_blocks), jnp.int32)],
        name="plan",
    )(meta, place)


def column_factor(coeffs, potential, columns):
    slabs = potential.shape[0]
    slab = lax.broadcasted_iota(jnp.int32, (columns, 1), 0) // (columns // slabs)
    factor = jnp.zeros((columns, 1), jnp.float32)
    for s in range(slabs):
        factor = jnp.where(slab == s, coeffs[potential[s]], factor)
    return factor


def untouched_kernel(coeffs, potential, x_prev, density, x_next, density_out):
    value = -x_prev[...]
    rows = value.shape[0]
    slab = (pl.num_programs(0) * rows) // potential.shape[0]
    first = pl.program_id(0) * rows
    x_next[...] = value
    factor = coeffs[potential[first // slab]]
    density_out[...] = density[...] + factor * value


def untouched(coeffs, potential, x_prev, density, rows=8):
    columns, local_rows = x_prev.shape
    while columns // potential.shape[0] % rows:
        rows //= 2
    wide = pl.BlockSpec((rows, local_rows), lambda i: (i, 0))
    return pl.pallas_call(
        untouched_kernel,
        grid=(columns // rows,),
        out_shape=[jax.ShapeDtypeStruct(x_prev.shape, jnp.float32)] * 2,
        in_specs=[SMEM] * 2 + [wide, wide],
        out_specs=[wide, wide],
        name="untouched",
    )(coeffs, potential, x_prev, density)


def add_kernel(bound, segments, width, parts, *refs):
    table, coeffs, potential = refs[:3]
    arrived = refs[3 : 3 + parts]
    x_next, density_out, held_x, held_d, held_a, sems, sems_a = refs[5 + parts :]
    opening, closing = table[4, bound], table[4, bound + len(segments)]

    def copies(position, back):
        start = pl.multiple_of(table[0, position] * width, width)
        index = table[1, position] - opening
        result = []
        for number, (whole, held) in enumerate(((x_next, held_x), (density_out, held_d))):
            near, far = held.at[index], whole.at[:, pl.ds(start, width)]
            source, target = (near, far) if back else (far, near)
            result.append(pltpu.make_async_copy(source, target, sems.at[index, 2 * back + number]))
        return result

    def each(body):
        for number, (part, entry) in enumerate(segments):

            def step(position, carry, part=part, entry=entry):
                local = table[3, position]
                source = arrived[part]
                source = source.at[local] if entry is None else source.at[entry, local]
                index = position - opening
                body(position, pltpu.make_async_copy(source, held_a.at[index], sems_a.at[index]))
                return carry

            lax.fori_loop(table[4, bound + number], table[4, bound + number + 1], step, 0)

    def begin(position, arrival):
        @pl.when(table[1, position] == position)
        def _():
            for copy in copies(position, 0):
                copy.start()

        arrival.start()

    each(begin)
    factor = column_factor(coeffs, potential, x_next.shape[0])

    def fold(position, arrival):
        lead = table[1, position]

        @pl.when(lead == position)
        def _():
            for copy in copies(position, 0):
                copy.wait()

        arrival.wait()
        value = 2.0 * held_a[position - opening].astype(jnp.float32)
        held_x[lead - opening] += value
        held_d[lead - opening] += factor * value

        @pl.when(table[2, position] == 1)
        def _():
            for copy in copies(position, 1):
                copy.start()

    each(fold)

    def settle(position, carry):
        @pl.when(table[2, position] == 1)
        def _():
            for copy in copies(position, 1):
                copy.wait()

        return carry

    lax.fori_loop(opening, closing, settle, 0)


def add_arrived(table, coeffs, potential, chunks, x_next, density_out, bound, width):
    columns = x_next.shape[0]
    segments, arrived, items = [], [], 0
    for chunk in chunks:
        if len(chunk) == 1:
            segments += [(len(arrived), entry) for entry in range(chunk[0].shape[0])]
        else:
            segments += [(len(arrived) + entry, None) for entry in range(len(chunk))]
        arrived += chunk
        items += sum(array.size for array in chunk) // (columns * width)
    parts = len(arrived)
    return pl.pallas_call(
        functools.partial(add_kernel, bound, tuple(segments), width, parts),
        out_shape=[jax.ShapeDtypeStruct(x_next.shape, jnp.float32)] * 2,
        in_specs=[SMEM] * 3 + [ANY] * parts + [ANY, ANY],
        out_specs=[ANY, ANY],
        scratch_shapes=[
            pltpu.VMEM((items, columns, width), jnp.float32),
            pltpu.VMEM((items, columns, width), jnp.float32),
            pltpu.VMEM((items, columns, width), jnp.bfloat16),
            pltpu.SemaphoreType.DMA((items, 4)),
            pltpu.SemaphoreType.DMA((items,)),
        ],
        input_output_aliases={3 + parts: 0, 4 + parts: 1},
    )(table, coeffs, potential, *arrived, x_next, density_out)


def after(value, other):
    return lax.optimization_barrier((value, other))[0]


def work(x_now, x_prev, density, coeffs, potential, h_tiles, tile_rows, tile_cols, tile_counts):
    chips = lax.axis_size("chip")
    reds = lax.axis_size("red")
    per_red = chips // reds
    devices = 2 * chips * reds
    capacity, width = h_tiles.shape[1], h_tiles.shape[-1]
    row_blocks = x_now.shape[1] // width // (2 * per_red)
    sizes = chunk_sizes(capacity)
    directs = DIRECT[: len(sizes)]
    groups = tuple(g for g in (tuple(range(len(sizes) - 1)), (len(sizes) - 1,)) if g)
    place = jnp.stack([lax.axis_index("chip"), lax.axis_index("core"), lax.axis_index("red")])
    own_facts = jnp.concatenate([tile_rows, tile_cols, tile_counts], axis=1)
    facts = {d: flip_chip(own_facts, d) if d else own_facts for d in range(chips)}
    other = lax.ppermute(x_now, "core", [(0, 1), (1, 0)])

    base = 0
    gate = None
    landed = []
    for number, (size, direct) in enumerate(zip(sizes, directs)):
        own = h_tiles[0, base : base + size]
        if gate is not None:
            own, gate = lax.optimization_barrier((own, gate))
        pieces, gate = spread(own, chips)
        if number == 0:
            spoken = jnp.broadcast_to(after(own_facts, gate), (devices, own_facts.shape[1]))
            meta = lax.all_to_all(
                spoken, ("chip", "core", "red"), split_axis=0, concat_axis=0, tiled=True
            )
            table = plan(meta, place, sizes, directs, groups, reds, per_red, capacity, row_blocks)
        result = products(
            place, x_now, other, facts, pieces, chips, reds, capacity, base, size, per_red, direct
        )
        if direct:
            blocks = [result[0]]
            for away in range(1, 2 * reds):
                blocks.append(flip_slice(result[away], away))
            landed.append(blocks)
        else:
            landed.append(
                [lax.all_to_all(result, ("core", "red"), split_axis=0, concat_axis=0, tiled=True)]
            )
        base += size
    x_next, density_out = untouched(coeffs, potential, x_prev, density)
    for group in groups:
        x_next, density_out = add_arrived(
            table,
            coeffs,
            potential,
            [landed[chunk] for chunk in group],
            x_next,
            density_out,
            2 * reds * group[0],
            width,
        )
    return x_next, density_out


def solution(mesh):
    blk, red = mesh.shape["blk"], mesh.shape["red"]
    chips = blk // 2
    split = Mesh(mesh.devices.reshape(chips, 2, red), ("chip", "core", "red"))
    rows = ("chip", "core")
    both = P(rows, "red")
    in_specs = (both, both, both, P(), P(rows), P(rows, "red", None, None), both, both, both)
    return jax.shard_map(
        work, mesh=split, in_specs=in_specs, out_specs=(both, both), check_vma=False
    )
```
